32 devices in a mesh: fsdp: 4 (over y, x), dp: 8 (over z, core).
Axes of the slice: x: 2, y: 2, z: 4, core: 2. Of those that a mesh axis runs over, the one named last changes fastest.
Arguments:
- tokens: bfloat16 [16, 1024, 896], P('dp', 'fsdp'), may hold values from -6 to 6
- segments: int32 [16, 1024], P('dp', 'fsdp'), may hold values from 0 to 3, never falling along the last dimension, each value on 1 to 512 neighbouring positions
- cotangent: bfloat16 [16, 1024, 896], P('dp', 'fsdp'), may hold values from -6 to 6
- norm_attn: bfloat16 [2, 896], P(None, 'fsdp'), may hold values from 0.099609375 to 1.8984375
- query_weight: bfloat16 [2, 896, 896], P(None, 'fsdp'), may hold values from -0.1875 to 0.1875
- query_bias: bfloat16 [2, 896], P(None, 'fsdp'), may hold values from -3 to 3
- key_weight: bfloat16 [2, 896, 128], P(None, 'fsdp'), may hold values from -0.1875 to 0.1875
- key_bias: bfloat16 [2, 128], P(None, 'fsdp'), may hold values from -3 to 3
- value_weight: bfloat16 [2, 896, 128], P(None, 'fsdp'), may hold values from -0.1875 to 0.1875
- value_bias: bfloat16 [2, 128], P(None, 'fsdp'), may hold values from -3 to 3
- out_weight: bfloat16 [2, 896, 896], P(None, 'fsdp'), may hold values from -1.5 to 1.5
- norm_mlp: bfloat16 [2, 896], P(None, 'fsdp'), may hold values from 0.099609375 to 1.8984375
- gate_weight: bfloat16 [2, 896, 4864], P(None, 'fsdp'), may hold values from -0.1875 to 0.1875
- up_weight: bfloat16 [2, 896, 4864], P(None, 'fsdp'), may hold values from -0.1875 to 0.1875
- down_weight: bfloat16 [2, 4864, 896], P(None, 'fsdp'), may hold values from -0.078125 to 0.078125
Outputs:
- out_tokens: bfloat16 [16, 1024, 896], P('dp', 'fsdp')
- grad_tokens: float32 [16, 1024, 896], P('dp', 'fsdp')
- grad_norm_attn: float32 [2, 896], P(None, 'fsdp')
- grad_query_weight: float32 [2, 896, 896], P(None, 'fsdp')
- grad_query_bias: float32 [2, 896], P(None, 'fsdp')
- grad_key_weight: float32 [2, 896, 128], P(None, 'fsdp')
- grad_key_bias: float32 [2, 128], P(None, 'fsdp')
- grad_value_weight: float32 [2, 896, 128], P(None, 'fsdp')
- grad_value_bias: float32 [2, 128], P(None, 'fsdp')
- grad_out_weight: float32 [2, 896, 896], P(None, 'fsdp')
- grad_norm_mlp: float32 [2, 896], P(None, 'fsdp')
- grad_gate_weight: float32 [2, 896, 4864], P(None, 'fsdp')
- grad_up_weight: float32 [2, 896, 4864], P(None, 'fsdp')
- grad_down_weight: float32 [2, 4864, 896], P(None, 'fsdp')
The draws below stay inside these ranges and needn't reach their ends.
Inputs may be any that keep to these rules, and one draw needn't show every extreme that they name: `segments`: within each sequence the document numbers never fall; each of the 4 documents has 1 to 512 tokens and one has exactly 512.
All inputs are finite; a program needn't handle non-finite values.
Results may differ from the reference program's by a relative error of at most 0.03.
Values may be sent and summed in bfloat16 or wider, within the bound.
No kernel may reach another device: no remote copies, remote signals or barrier semaphores. Data moves between devices by JAX's collectives and lax.ppermute only.
A program may use at most 384 MiB of HBM per device.

```python
import math
import jax
import jax.numpy as jnp
import numpy as np
from jax import lax

D = 896
FF = 4864
HEADS = 14
KV_HEADS = 2
HD = 64
LAYERS = 2
SEQ = 1024
QW = 896
KVW = 128
SEQS = 16


def level_of(rng, shape, cuts, smallest, largest):
    gain = 1.0
    for axis_at, blocks in cuts:
        draws = jax.random.uniform(jax.random.fold_in(jax.random.fold_in(rng, 6), axis_at), (blocks,), jnp.float32, smallest / len(cuts), largest / len(cuts))
        gain = gain * jnp.repeat(jnp.exp(draws), shape[axis_at] // blocks).reshape((-1,) + (1,) * (len(shape) - 1 - axis_at))
    return gain


def split_up(number_of, total, limit, slope):
    weights = [(1 << 20) // math.isqrt(grade ** slope) + 1 for grade in range(2, number_of + 1)]
    spare, holding = total - limit - (number_of - 1), [1] * (number_of - 1)
    while spare > 0:
        free = [i for i in range(number_of - 1) if holding[i] < limit]
        whole, remaining = sum([weights[i] for i in free]), spare
        for i in free:
            addition = min(limit - holding[i], max(1, remaining * weights[i] // whole), spare)
            holding[i] = holding[i] + addition
            spare = spare - addition
    return np.array([limit] + holding)


def ragged(key, number_of, total, reach, lean):
    if number_of == 2:
        one = jax.random.randint(key, (), max(1, total - reach), min(reach, total - 1) + 1)
        return jnp.stack([one, total - one])
    sizes = jnp.asarray(split_up(number_of, total, reach, lean), jnp.int32)
    couples = (number_of - 1) // 2
    donor, sink = sizes[1:1 + 2 * couples:2], sizes[2:2 + 2 * couples:2]
    slack = jnp.minimum(donor - 1, reach - sink)
    moved = jax.random.randint(jax.random.fold_in(key, 1), (couples,), 0, 1 << 20) % (slack + 1)
    sizes = sizes.at[1:1 + 2 * couples:2].set(donor - moved).at[2:2 + 2 * couples:2].set(sink + moved)
    return sizes[jax.random.permutation(jax.random.fold_in(key, 2), number_of)]


def noise(key, extent, width, reach, shards=(), kind=jnp.bfloat16):
    drawn = width * jax.random.normal(key, extent, jnp.float32)
    if shards:
        drawn = drawn * level_of(key, extent, shards, -0.22, 0.18)
    return jnp.clip(drawn, -reach, reach).astype(kind)


def setup_inputs(seed: int = 0) -> dict:
    keys = jax.random.split(jax.random.key(seed), 16)
    return {
        "tokens": noise(keys[0], (SEQS, SEQ, D), 1.0, 6.0, ((0, 8), (1, 4))),
        "segments": jax.vmap(lambda own: jnp.searchsorted(jnp.cumsum(ragged(own, 4, SEQ, SEQ // 2, 0)), jnp.arange(SEQ), side="right"))(jax.random.split(keys[1], SEQS)).reshape((SEQS, SEQ)).astype(jnp.int32),
        "cotangent": noise(keys[2], (SEQS, SEQ, D), 1.0, 6.0, ((0, 8), (1, 4))),
        "norm_attn": jnp.clip(1.0 + 0.18 * jax.random.normal(keys[3], (LAYERS, D), jnp.float32), 0.099609375, 1.8984375).astype(jnp.bfloat16),
        "query_weight": noise(keys[4], (LAYERS, D, QW), D ** -0.5, 0.1875, ((1, 4),)),
        "query_bias": noise(keys[5], (LAYERS, QW), 0.5, 3.0, ((1, 4),)),
        "key_weight": noise(keys[6], (LAYERS, D, KVW), D ** -0.5, 0.1875, ((1, 4),)),
        "key_bias": noise(keys[7], (LAYERS, KVW), 0.5, 3.0, ((1, 4),)),
        "value_weight": noise(keys[8], (LAYERS, D, KVW), D ** -0.5, 0.1875, ((1, 4),)),
        "value_bias": noise(keys[9], (LAYERS, KVW), 0.5, 3.0, ((1, 4),)),
        "out_weight": noise(keys[10], (LAYERS, QW, D), (D // 64) ** -0.5, 1.5, ((1, 4),)),
        "norm_mlp": jnp.clip(1.0 + 0.18 * jax.random.normal(keys[11], (LAYERS, D), jnp.float32), 0.099609375, 1.8984375).astype(jnp.bfloat16),
        "gate_weight": noise(keys[12], (LAYERS, D, FF), D ** -0.5, 0.1875, ((1, 4),)),
        "up_weight": noise(keys[13], (LAYERS, D, FF), D ** -0.5, 0.1875, ((1, 4),)),
        "down_weight": noise(keys[14], (LAYERS, FF, D), FF ** -0.5, 0.078125, ((1, 4),)),
    }


@jax.custom_vjp
def low(v):
    return lax.optimization_barrier(v.astype(jnp.bfloat16)).astype(jnp.float32)

@jax.custom_vjp
def low_back(v):
    return v

def low_keep(v):
    return (low(v), None)

def low_pass(kept, grad):
    return (grad,)

def back_keep(v):
    return (v, None)

def back_low(kept, grad):
    return (low(grad),)
low.defvjp(low_keep, low_pass)
low_back.defvjp(back_keep, back_low)
EPS = 1e-06
THETA = 1000000.0
PRECISE = lax.Precision.HIGHEST

def matmul(former, latter):
    return jnp.einsum('...i,ij->...j', former, latter, precision=PRECISE)

def rms_apply(stream, gain_vec):
    factor = lax.rsqrt(lax.optimization_barrier(jnp.mean(stream * stream, -1, keepdims=True)) + EPS)
    return stream * factor * gain_vec

def rope_tables(positions):
    half_dim = HD // 2
    inverse = THETA ** (-(jnp.arange(half_dim, dtype=jnp.float32) * 2.0) / HD)
    angles = positions[..., None].astype(jnp.float32) * inverse
    angles = jnp.concatenate([angles, angles], -1)
    return (jnp.cos(angles)[..., None, :], jnp.sin(angles)[..., None, :])

def rotate(vectors, cosine, sine):
    half_dim = vectors.shape[-1] // 2
    turned = jnp.concatenate([-vectors[..., half_dim:], vectors[..., :half_dim]], -1)
    return vectors * cosine + turned * sine

def attend_block(queries, key_set, value_set, seg_rows, seg_all, row_ids):
    row_count = queries.shape[0]
    grouped = queries.reshape(row_count, KV_HEADS, HEADS // KV_HEADS, HD)
    scores = low_back(jnp.einsum('tkgd,skd->kgts', grouped, key_set, precision=PRECISE)) * (1.0 / math.sqrt(HD))
    col_ids = jnp.arange(key_set.shape[0], dtype=jnp.int32)
    allowed = (seg_rows[:, None] == seg_all[None, :]) & (col_ids[None, :] <= row_ids[:, None])
    scores = jnp.where(allowed, scores, -1000000000.0)
    shares = low(jax.nn.softmax(scores, axis=-1))
    output = jnp.einsum('kgts,skd->tkgd', shares, value_set, precision=PRECISE)
    return output.reshape(row_count, HEADS * HD)

def attention(queries, key_set, value_set, segments):
    block_len = min(512, SEQ)
    blocks = SEQ // block_len
    checked = jax.checkpoint(attend_block)

    def one_sequence(bundle):
        query_seq, keys_seq, values_seq, seg_seq = bundle
        row_ids = jnp.arange(SEQ, dtype=jnp.int32).reshape(blocks, block_len)

        def one_block(portion):
            return checked(portion[0], keys_seq, values_seq, portion[1], seg_seq, portion[2])
        results = lax.map(one_block, (query_seq.reshape(blocks, block_len, HEADS, HD), seg_seq.reshape(blocks, block_len), row_ids))
        return results.reshape(SEQ, HEADS * HD)
    return lax.map(one_sequence, (queries, key_set, value_set, segments))

def block_forward(stream, weights, cosine, sine, segments):
    gain_in, query_weight, query_bias, key_weight, key_bias, value_weight, value_bias, out_weight, gain_mid, gate_weight, up_weight, down_weight = weights
    normed = low(rms_apply(stream, gain_in))
    query_raw = low_back(matmul(normed, query_weight) + query_bias)
    key_raw = low_back(matmul(normed, key_weight) + key_bias)
    value_raw = low(low_back(matmul(normed, value_weight) + value_bias))
    shape_lead = stream.shape[:-1]
    queries = low(rotate(query_raw.reshape(shape_lead + (HEADS, HD)), cosine, sine))
    key_set = low(rotate(key_raw.reshape(shape_lead + (KV_HEADS, HD)), cosine, sine))
    value_set = value_raw.reshape(shape_lead + (KV_HEADS, HD))
    attended = low(low_back(attention(queries, key_set, value_set, segments)))
    stream_mid = stream + low_back(matmul(attended, out_weight))
    normed_mid = low(rms_apply(stream_mid, gain_mid))
    gate = low_back(matmul(normed_mid, gate_weight))
    upward = low_back(matmul(normed_mid, up_weight))
    hidden = low(jax.nn.silu(gate) * upward)
    return stream_mid + low_back(matmul(hidden, down_weight))

def reference(tokens, segments, cotangent, norm_attn, query_weight, query_bias, key_weight, key_bias, value_weight, value_bias, out_weight, norm_mlp, gate_weight, up_weight, down_weight):
    weights = tuple((array.astype(jnp.float32) for array in (norm_attn, query_weight, query_bias, key_weight, key_bias, value_weight, value_bias, out_weight, norm_mlp, gate_weight, up_weight, down_weight)))
    row_ids = jnp.arange(SEQ, dtype=jnp.int32)
    starts = lax.optimization_barrier(jnp.sum((segments[:, None, :] < segments[:, :, None]).astype(jnp.int32), axis=-1))
    cosine, sine = rope_tables(row_ids[None, :] - starts)

    def forward(stream, params):
        for layer_at in range(LAYERS):
            stream = block_forward(stream, tuple((array[layer_at] for array in params)), cosine, sine, segments)
        return stream
    result, pull = jax.vjp(forward, tokens.astype(jnp.float32), weights)
    grad_in, grads = pull(cotangent.astype(jnp.float32))
    return (result.astype(jnp.bfloat16), grad_in, grads[0], grads[1], grads[2], grads[3], grads[4], grads[5], grads[6], grads[7], grads[8], grads[9], grads[10], grads[11])
```

```python
import functools
import math

import jax
import jax.numpy as jnp
from jax import lax
from jax.experimental import pallas as pl
from jax.experimental.pallas import tpu as pltpu
from jax.sharding import PartitionSpec as P

HEADS = 14
KV_HEADS = 2
HD = 64
LAYERS = 2
QW = 896
KVW = 128
LANES = 128
PAIRS = HEADS // 2
GROUP = HEADS // KV_HEADS

EPS = 1e-06
THETA = 1000000.0
SCALE = 1.0 / math.sqrt(HD)
NEG = -1000000000.0


F32 = jnp.float32
BF16 = jnp.bfloat16


def lane_ids(shape):
    return lax.broadcasted_iota(jnp.int32, shape, len(shape) - 1)


def rope_lanes(values, cosine, sine):
    low_half = (lane_ids(values.shape) % HD) < HD // 2
    ahead = pltpu.roll(values, LANES - HD // 2, values.ndim - 1)
    behind = pltpu.roll(values, HD // 2, values.ndim - 1)
    return values * cosine + jnp.where(low_half, -ahead, behind) * sine


def rope_back_lanes(values, cosine, sine):
    low_half = (lane_ids(values.shape) % HD) < HD // 2
    moved = values * sine
    ahead = pltpu.roll(moved, LANES - HD // 2, values.ndim - 1)
    behind = pltpu.roll(moved, HD // 2, values.ndim - 1)
    return values * cosine + jnp.where(low_half, ahead, -behind)


def pair_rows(rows, pair):
    low = lane_ids(rows.shape) < HD
    rows = rows.astype(F32)
    turned = pltpu.roll(rows, HD, 1)
    first = jnp.where(pair * 2 >= GROUP, turned, rows)
    second = jnp.where(pair * 2 + 1 >= GROUP, rows, turned)
    zero = jnp.zeros_like(rows)
    return jnp.where(low, first, zero).astype(BF16), jnp.where(low, zero, second).astype(BF16)


def dot_nn(former, latter):
    return lax.dot_general(former, latter, (((1,), (0,)), ((), ())), preferred_element_type=F32)


def dot_nt(former, latter):
    return lax.dot_general(former, latter, (((1,), (1,)), ((), ())), preferred_element_type=F32)


def dot_tn(former, latter):
    return lax.dot_general(former, latter, (((0,), (0,)), ((), ())), preferred_element_type=F32)


def attn_fwd_kernel(act, qraw, cosine, sine, k_all, v_all, seg_col, seg_row, q_out, o_out, lse_out, m_s, l_s, acc_s):
    pair = pl.program_id(0)
    parts, rows, _ = k_all.shape
    q = rope_lanes(qraw[...], cosine[...], sine[...]).astype(BF16)
    q_out[...] = q
    low = lane_ids((rows, LANES)) < HD
    for at in range(parts):

        def step(at=at):
            keys = pair_rows(k_all[at], pair)
            values = pair_rows(v_all[at], pair)
            mask = seg_col[...] == seg_row[at]
            if at == 0:
                shape = (rows, rows)
                mask = mask & (lax.broadcasted_iota(jnp.int32, shape, 1) <= lax.broadcasted_iota(jnp.int32, shape, 0))
            tops, sums, fresh = [], [], None
            for side in range(2):
                scores = jnp.where(mask, dot_nt(q, keys[side]) * SCALE, NEG)
                top = jnp.max(scores, -1, keepdims=True)
                if at > 0:
                    top = jnp.maximum(top, m_s[:, side * HD : side * HD + 1])
                shares = jnp.exp(scores - top)
                tops.append(top)
                sums.append(jnp.sum(shares, -1, keepdims=True))
                part = dot_nn(shares.astype(BF16), values[side])
                fresh = part if fresh is None else fresh + part
            top = jnp.where(low, tops[0], tops[1])
            total = jnp.where(low, sums[0], sums[1])
            if at > 0:
                keep = jnp.exp(m_s[...] - top)
                total = total + l_s[...] * keep
                fresh = fresh + acc_s[...] * keep
            m_s[...] = top
            l_s[...] = total
            acc_s[...] = fresh

        if at == 0:
            step()
        else:
            pl.when(act[at] > 0)(step)
    o_out[...] = (acc_s[...] / l_s[...]).astype(BF16)
    lse_out[...] = m_s[...] + jnp.log(l_s[...])


def attn_fwd(act, qraw, cosine, sine, k_all, v_all, seg_col, seg_row):
    parts, rows, _ = k_all.shape
    block = pl.BlockSpec((rows, LANES), lambda p, a: (0, p))
    same = pl.BlockSpec((rows, LANES), lambda p, a: (0, 0))
    kv = pl.BlockSpec((parts, rows, LANES), lambda p, a: (0, 0, 0))
    scores = HEADS * rows * parts * rows
    return pl.pallas_call(
        attn_fwd_kernel,
        grid_spec=pltpu.PrefetchScalarGridSpec(
            num_scalar_prefetch=1,
            grid=(PAIRS,),
            in_specs=[
                block,
                same,
                same,
                kv,
                kv,
                pl.BlockSpec((rows, 1), lambda p, a: (0, 0)),
                pl.BlockSpec((parts, 1, rows), lambda p, a: (0, 0, 0)),
            ],
            out_specs=[block, block, pl.BlockSpec((None, rows, LANES), lambda p, a: (p, 0, 0))],
            scratch_shapes=[pltpu.VMEM((rows, LANES), F32)] * 3,
        ),
        out_shape=(
            jax.ShapeDtypeStruct((rows, QW), BF16),
            jax.ShapeDtypeStruct((rows, QW), BF16),
            jax.ShapeDtypeStruct((PAIRS, rows, LANES), F32),
        ),
        cost_estimate=pl.CostEstimate(flops=scores * 512, bytes_accessed=rows * QW * 12, transcendentals=scores),
        name="attn_fwd",
    )(act, qraw, cosine, sine, k_all, v_all, seg_col, seg_row)


def attn_bwd_kernel(
    act, q_in, do_in, lse_in, cosine, sine, k_all, v_all, seg_col, seg_row, dq_out, dk_out, dv_out, dk_s, dv_s, dq_s, inner_s, share_s, grad_s
):
    pair = pl.program_id(0)
    parts, rows, _ = k_all.shape
    kind = jnp.where(pair * 2 + 1 >= GROUP, 1, 0) + jnp.where(pair * 2 >= GROUP, 1, 0)
    low = lane_ids((rows, LANES)) < HD

    @pl.when(pair == 0)
    def _():
        dk_s[...] = jnp.zeros_like(dk_s)
        dv_s[...] = jnp.zeros_like(dv_s)

    q = q_in[...]
    do = do_in[...]
    lse_t = jnp.transpose(lse_in[...])
    dq_s[...] = jnp.zeros_like(dq_s)
    inner_s[...] = jnp.zeros_like(inner_s)

    def shares_of(at):
        keys = pair_rows(k_all[at], pair)
        values = pair_rows(v_all[at], pair)
        mask = seg_col[at] == seg_row[...]
        if at == 0:
            shape = (rows, rows)
            mask = mask & (lax.broadcasted_iota(jnp.int32, shape, 0) <= lax.broadcasted_iota(jnp.int32, shape, 1))
        dvs = []
        for side in range(2):
            scores = jnp.where(mask, dot_nt(keys[side], q) * SCALE, NEG)
            shares = jnp.exp(scores - lse_t[side * HD : side * HD + 1, :])
            grad_share = dot_nt(values[side], do)
            inner_s[side : side + 1, :] += jnp.sum(shares * grad_share, 0, keepdims=True)
            share_s[at, side] = shares
            grad_s[at, side] = grad_share
            dvs.append(dot_nn(shares.astype(BF16), do))
        dv_s[kind, at] += jnp.where(low, dvs[0], dvs[1])

    def scores_of(at):
        keys = pair_rows(k_all[at], pair)
        dks = []
        for side in range(2):
            grad_score = (share_s[at, side] * (grad_s[at, side] - inner_s[side : side + 1, :]) * SCALE).astype(BF16)
            dks.append(dot_nn(grad_score, q))
            dq_s[...] += dot_tn(grad_score, keys[side])
        dk_s[kind, at] += jnp.where(low, dks[0], dks[1])

    for stage in (shares_of, scores_of):
        for at in range(parts):
            if at == 0:
                stage(at)
            else:
                pl.when(act[at] > 0)(functools.partial(stage, at))
    dq_out[...] = rope_back_lanes(dq_s[...], cosine[...], sine[...]).astype(BF16)

    @pl.when(pair == PAIRS - 1)
    def _():
        for at in range(parts):
            for acc, out in ((dk_s, dk_out), (dv_s, dv_out)):
                both_low, split, both_high = acc[0, at], acc[1, at], acc[2, at]
                folded_low = both_low + pltpu.roll(both_low, HD, 1)
                folded_high = both_high + pltpu.roll(both_high, HD, 1)
                out[at] = (split + jnp.where(low, folded_low, folded_high)).astype(BF16)


def attn_bwd(act, q, do, lse, cosine, sine, k_all, v_all, seg_col, seg_row):
    parts, rows, _ = k_all.shape
    block = pl.BlockSpec((rows, LANES), lambda p, a: (0, p))
    same = pl.BlockSpec((rows, LANES), lambda p, a: (0, 0))
    kv = pl.BlockSpec((parts, rows, LANES), lambda p, a: (0, 0, 0))
    scores = HEADS * rows * parts * rows
    return pl.pallas_call(
        attn_bwd_kernel,
        grid_spec=pltpu.PrefetchScalarGridSpec(
            num_scalar_prefetch=1,
            grid=(PAIRS,),
            in_specs=[
                block,
                block,
                pl.BlockSpec((None, rows, LANES), lambda p, a: (p, 0, 0)),
                same,
                same,
                kv,
                kv,
                pl.BlockSpec((parts, rows, 1), lambda p, a: (0, 0, 0)),
                pl.BlockSpec((1, rows), lambda p, a: (0, 0)),
            ],
            out_specs=[block, kv, kv],
            scratch_shapes=[
                pltpu.VMEM((3, parts, rows, LANES), F32),
                pltpu.VMEM((3, parts, rows, LANES), F32),
                pltpu.VMEM((rows, LANES), F32),
                pltpu.VMEM((2, rows), F32),
                pltpu.VMEM((parts, 2, rows, rows), F32),
                pltpu.VMEM((parts, 2, rows, rows), F32),
            ],
        ),
        out_shape=(
            jax.ShapeDtypeStruct((rows, QW), BF16),
            jax.ShapeDtypeStruct((parts, rows, LANES), BF16),
            jax.ShapeDtypeStruct((parts, rows, LANES), BF16),
        ),
        cost_estimate=pl.CostEstimate(flops=scores * 1280, bytes_accessed=rows * QW * 12, transcendentals=scores),
        name="attn_bwd",
    )(act, q, do, lse, cosine, sine, k_all, v_all, seg_col, seg_row)


def swap(values, axis, bits):
    return lax.ppermute(values, axis, [(i, i ^ bits) for i in range(lax.axis_size(axis))])


def gather_rel(own):
    parts = lax.axis_size("fsdp")
    if parts == 4:
        half = own.shape[0] // 2
        by_x, by_y = swap(own, "fsdp", 1), swap(own, "fsdp", 2)
        top = swap(by_y[:half], "fsdp", 1)
        bottom = swap(by_x[half:], "fsdp", 2)
        return [own, by_x, by_y, jnp.concatenate([top, bottom])]
    return [own] + [swap(own, "fsdp", s) for s in range(1, parts)]


def scatter_rel(pieces):
    parts = len(pieces)
    if parts == 4:
        half = pieces[3].shape[0] // 2
        via_x = swap(pieces[3][:half], "fsdp", 1)
        via_y = swap(pieces[3][half:], "fsdp", 2)
        to_y = jnp.concatenate([(pieces[2][:half].astype(F32) + via_x.astype(F32)).astype(BF16), pieces[2][half:]])
        to_x = jnp.concatenate([pieces[1][:half], (pieces[1][half:].astype(F32) + via_y.astype(F32)).astype(BF16)])
        got = [swap(to_x, "fsdp", 1), swap(to_y, "fsdp", 2)]
    else:
        got = [swap(pieces[s], "fsdp", s) for s in range(1, parts)]
    total = pieces[0].astype(F32)
    for piece in got:
        total = total + piece.astype(F32)
    return total


def exchange_rel(pieces):
    return [pieces[0]] + [swap(pieces[s], "fsdp", s) for s in range(1, len(pieces))]


def place(rel, me):
    out = jnp.zeros((len(rel),) + rel[0].shape, rel[0].dtype)
    for s, block in enumerate(rel):
        out = lax.dynamic_update_index_in_dim(out, block, me ^ s, 0)
    return out


def pick(stacked, index):
    return lax.dynamic_index_in_dim(stacked, index, 0, keepdims=False)


def line_sum(values, at):
    count = lax.axis_size("dp")
    if count == 8:
        chip = at // 2
        ends = (chip == 0) | (chip == 3)
        inward = lax.ppermute(values, "dp", [(0, 2), (1, 3), (6, 4), (7, 5)])
        held = (values.astype(F32) + inward.astype(F32)).astype(BF16)
        across = lax.ppermute(held, "dp", [(2, 4), (3, 5), (4, 2), (5, 3)])
        total = (held.astype(F32) + across.astype(F32)).astype(BF16)
        outward = lax.ppermute(total, "dp", [(2, 0), (3, 1), (4, 6), (5, 7)])
        return jnp.where(ends, outward, total)
    bits = 2
    while bits < count:
        values = (values.astype(F32) + swap(values, "dp", bits).astype(F32)).astype(BF16)
        bits *= 2
    return values


def core_half(stacked, core):
    mine, other = pick(stacked, core), pick(stacked, 1 - core)
    return (mine.astype(F32) + swap(other, "dp", 1).astype(F32)).astype(BF16)


def core_join(half, core):
    other = swap(half, "dp", 1)
    first = jnp.where(core == 0, half, other)
    second = jnp.where(core == 0, other, half)
    return first, second


def rms_parts(stream):
    return lax.rsqrt(jnp.mean(stream * stream, -1, keepdims=True) + EPS)


def rms_back(stream, gain, grad):
    factor = rms_parts(stream)
    scaled = grad * gain
    grad_gain = jnp.sum(grad * stream * factor, 0)
    inner = jnp.mean(stream * scaled, -1, keepdims=True)
    return grad_gain, factor * scaled - stream * (factor * factor * factor * inner)


def rope_keys(values, cosine, sine):
    half = HD // 2
    turned = jnp.concatenate(
        [-values[:, half:HD], values[:, :half], -values[:, HD + half :], values[:, HD : HD + half]], -1
    )
    return values * cosine + turned * sine


def rope_keys_back(values, cosine, sine):
    half = HD // 2
    moved = values * sine
    turned = jnp.concatenate(
        [moved[:, half:HD], -moved[:, :half], moved[:, HD + half :], -moved[:, HD : HD + half]], -1
    )
    return values * cosine + turned


def body(
    tokens,
    segments,
    cotangent,
    norm_attn,
    query_weight,
    query_bias,
    key_weight,
    key_bias,
    value_weight,
    value_bias,
    out_weight,
    norm_mlp,
    gate_weight,
    up_weight,
    down_weight,
):
    seqs, rows = segments.shape
    parts = lax.axis_size("fsdp")
    me = lax.axis_index("fsdp")
    at = lax.axis_index("dp")
    core = at % 2
    width = tokens.shape[2]
    own_rows = width // parts
    own_ff = down_weight.shape[1]
    half_rows = own_rows // 2

    seg_rel = jnp.stack([segments] + [swap(segments, "fsdp", s) for s in range(1, parts)])
    starts = jnp.sum((seg_rel[:, :, None, :] < segments[None, :, :, None]).astype(jnp.int32), axis=(0, 3))
    positions = me * rows + jnp.arange(rows, dtype=jnp.int32)[None, :] - starts
    inverse = THETA ** (-(jnp.arange(HD // 2, dtype=F32) * 2.0) / HD)
    angles = positions[..., None].astype(F32) * jnp.tile(inverse, LANES // (HD // 2))
    cosine, sine = jnp.cos(angles), jnp.sin(angles)
    blocks = me ^ jnp.arange(parts, dtype=jnp.int32)
    active = ((blocks[None, :] <= me) & ((blocks[None, :] + 1) * rows > starts[:, :1])).astype(jnp.int32)

    small = jnp.concatenate([norm_attn, query_bias, norm_mlp, key_bias, value_bias], 1)
    small_all = place([small] + [swap(small, "fsdp", s) for s in range(1, parts)], me)
    edges = [0]
    for array in (norm_attn, query_bias, norm_mlp, key_bias, value_bias):
        edges.append(edges[-1] + array.shape[1])

    def vector(position, layer_at):
        return small_all[:, layer_at, edges[position] : edges[position + 1]].reshape(-1).astype(F32)

    def gather_rows(weight):
        mine = lax.dynamic_slice_in_dim(weight, core * half_rows, half_rows, 0)
        fetched = place(gather_rel(mine), me)
        first, second = core_join(fetched, core)
        return jnp.stack([first, second], 1).reshape(width, weight.shape[1])

    def spread_columns(weight):
        mine = lax.dynamic_slice_in_dim(weight, core * half_rows, half_rows, 0)
        pieces = [lax.dynamic_slice_in_dim(mine, (me ^ s) * own_ff, own_ff, 1) for s in range(parts)]
        fetched = place(exchange_rel(pieces), me)
        first, second = core_join(fetched, core)
        return jnp.stack([first, second], 1).reshape(width, own_ff)

    weights = []
    for layer_at in range(LAYERS):
        wqkv = gather_rows(
            jnp.concatenate([query_weight[layer_at], key_weight[layer_at], value_weight[layer_at]], 1)
        )
        wout = gather_rows(out_weight[layer_at])
        wgate = spread_columns(gate_weight[layer_at])
        wup = spread_columns(up_weight[layer_at])
        weights.append((wqkv, wout, wgate, wup, down_weight[layer_at]))

    stream = [tokens[s].astype(F32) for s in range(seqs)]
    saved = [[None] * seqs for _ in range(LAYERS)]
    for layer_at in range(LAYERS):
        wqkv, wout, wgate, wup, wdown = weights[layer_at]
        gain_in, gain_mid = vector(0, layer_at), vector(2, layer_at)
        bias = jnp.concatenate([vector(1, layer_at), vector(3, layer_at), vector(4, layer_at)])
        for s in range(seqs):
            x0 = stream[s]
            normed = (x0 * rms_parts(x0) * gain_in).astype(BF16)
            raw = dot_nn(normed, wqkv) + bias
            keys = rope_keys(raw[:, QW : QW + KVW], cosine[s], sine[s]).astype(BF16)
            values = raw[:, QW + KVW :].astype(BF16)
            kv_rel = jnp.stack(gather_rel(jnp.concatenate([keys, values], 1)))
            k_rel, v_rel = kv_rel[:, :, :KVW], kv_rel[:, :, KVW:]
            q, o, lse = attn_fwd(
                active[s],
                raw[:, :QW],
                cosine[s],
                sine[s],
                k_rel,
                v_rel,
                segments[s][:, None],
                seg_rel[:, s][:, None, :],
            )
            x1 = x0 + dot_nn(o, wout)
            normed_mid = (x1 * rms_parts(x1) * gain_mid).astype(BF16)
            mid_all = jnp.concatenate(gather_rel(normed_mid))
            gate = dot_nn(mid_all, wgate)
            upward = dot_nn(mid_all, wup)
            hidden = (gate * jax.nn.sigmoid(gate) * upward).astype(BF16)
            partial = dot_nn(hidden, wdown).astype(BF16).reshape(parts, rows, width)
            stream[s] = x1 + scatter_rel([partial[i] for i in range(parts)])
            saved[layer_at][s] = (
                x0,
                normed,
                q,
                k_rel,
                v_rel,
                lse,
                o,
                x1,
                mid_all,
                gate.astype(BF16),
                upward.astype(BF16),
                hidden,
            )
    out_tokens = jnp.stack(stream).astype(BF16)

    def reduce_columns(total):
        shaped = total.astype(BF16).reshape(parts, 2, half_rows, own_ff).transpose(1, 0, 2, 3)
        half = core_half(shaped, core)
        pieces = exchange_rel([pick(half, me ^ s) for s in range(parts)])
        rows_half = place(pieces, me).transpose(1, 0, 2).reshape(half_rows, parts * own_ff)
        first, second = core_join(line_sum(rows_half, at), core)
        return jnp.concatenate([first, second]).astype(F32)

    def reduce_rows(total):
        half = core_half(total.astype(BF16).reshape(2, own_ff // 2, width), core)
        first, second = core_join(line_sum(half, at), core)
        return jnp.concatenate([first, second]).astype(F32)

    def reduce_packed(packed):
        half = core_half(packed.transpose(1, 0, 2, 3), core)
        own = scatter_rel([pick(half, me ^ s) for s in range(parts)]).astype(BF16)
        first, second = core_join(line_sum(own, at), core)
        return first.astype(F32), second.astype(F32)

    grad = [cotangent[s].astype(F32) for s in range(seqs)]
    results = [None] * LAYERS
    for layer_at in reversed(range(LAYERS)):
        wqkv, wout, wgate, wup, wdown = weights[layer_at]
        gain_in, gain_mid = vector(0, layer_at), vector(2, layer_at)
        sums = {}

        def add(name, value):
            sums[name] = value if name not in sums else sums[name] + value

        grad_mids = []
        for s in range(seqs):
            x1, mid_all, gate, upward, hidden = saved[layer_at][s][7:]
            grad_all = jnp.concatenate(gather_rel(grad[s].astype(BF16)))
            grad_hidden = dot_nt(grad_all, wdown)
            gate, upward = gate.astype(F32), upward.astype(F32)
            sig = jax.nn.sigmoid(gate)
            grad_gate = (grad_hidden * upward * (sig * (1.0 + gate * (1.0 - sig)))).astype(BF16)
            grad_up = (grad_hidden * (gate * sig)).astype(BF16)
            partial = (dot_nt(grad_gate, wgate) + dot_nt(grad_up, wup)).astype(BF16).reshape(parts, rows, width)
            add("down", dot_tn(hidden, grad_all))
            add("gate", dot_tn(mid_all, grad_gate))
            add("up", dot_tn(mid_all, grad_up))
            grad_normed = scatter_rel([partial[i] for i in range(parts)])
            gain_grad, grad_part = rms_back(x1, gain_mid, grad_normed)
            add("gain_mid", gain_grad)
            grad_mids.append(grad[s] + grad_part)
        down_grad = reduce_rows(sums["down"])
        gate_grad = reduce_columns(sums["gate"])
        up_grad = reduce_columns(sums["up"])
        for s in range(seqs):
            x0, normed, q, k_rel, v_rel, lse, o = saved[layer_at][s][:7]
            grad_mid = grad_mids[s]
            branch = grad_mid.astype(BF16)
            grad_att = dot_nt(branch, wout).astype(BF16)
            dq, dk, dv = attn_bwd(
                active[s],
                q,
                grad_att,
                lse,
                cosine[s],
                sine[s],
                k_rel,
                v_rel,
                seg_rel[:, s][:, :, None],
                segments[s][None, :],
            )
            dkv = jnp.concatenate([dk, dv], 2)
            dkv_own = scatter_rel([dkv[i] for i in range(parts)])
            dk_own = rope_keys_back(dkv_own[:, :KVW], cosine[s], sine[s])
            dqkv = jnp.concatenate([dq, dk_own.astype(BF16), dkv_own[:, KVW:].astype(BF16)], 1)
            add("out", dot_tn(o, branch))
            add("qkv", dot_tn(normed, dqkv))
            add("bias", jnp.sum(dqkv.astype(F32), 0))
            gain_grad, grad_part = rms_back(x0, gain_in, dot_nt(dqkv, wqkv))
            add("gain_in", gain_grad)
            grad[s] = grad_mid + grad_part
        columns = QW + 2 * KVW + width
        packed = jnp.concatenate([sums["qkv"], sums["out"]], 1).reshape(parts, own_rows, columns)
        bias = sums["bias"]
        vectors = jnp.concatenate(
            [
                sums["gain_in"].reshape(parts, -1),
                bias[:QW].reshape(parts, -1),
                sums["gain_mid"].reshape(parts, -1),
                bias[QW : QW + KVW].reshape(parts, -1),
                bias[QW + KVW :].reshape(parts, -1),
            ],
            1,
        )
        spare = jnp.pad(vectors[:, None, :], ((0, 0), (0, 31), (0, columns - vectors.shape[1])))
        halves = jnp.stack(
            [
                jnp.concatenate([packed[:, :half_rows], spare[:, :16]], 1),
                jnp.concatenate([packed[:, half_rows:], spare[:, 16:]], 1),
            ],
            1,
        )
        first, second = reduce_packed(halves.astype(BF16))
        matrix = jnp.concatenate([first[:half_rows], second[:half_rows]])
        vec = first[half_rows]
        results[layer_at] = (
            vec[edges[0] : edges[1]],
            matrix[:, :QW],
            vec[edges[1] : edges[2]],
            matrix[:, QW : QW + KVW],
            vec[edges[3] : edges[4]],
            matrix[:, QW + KVW : QW + 2 * KVW],
            vec[edges[4] : edges[5]],
            matrix[:, QW + 2 * KVW :],
            vec[edges[2] : edges[3]],
            gate_grad,
            up_grad,
            down_grad,
        )
    stacked = [jnp.stack([results[layer_at][i] for layer_at in range(LAYERS)]) for i in range(12)]
    return (out_tokens, jnp.stack(grad), *stacked)


def solution(mesh):
    rows3 = P("dp", "fsdp", None)
    return jax.shard_map(
        body,
        mesh=mesh,
        in_specs=(
            rows3,
            P("dp", "fsdp"),
            rows3,
            P(None, "fsdp"),
            P(None, "fsdp", None),
            P(None, "fsdp"),
            P(None, "fsdp", None),
            P(None, "fsdp"),
            P(None, "fsdp", None),
            P(None, "fsdp"),
            P(None, "fsdp", None),
            P(None, "fsdp"),
            P(None, "fsdp", None),
            P(None, "fsdp", None),
            P(None, "fsdp", None),
        ),
        out_specs=(
            rows3,
            rows3,
            P(None, "fsdp"),
            P(None, "fsdp", None),
            P(None, "fsdp"),
            P(None, "fsdp", None),
            P(None, "fsdp"),
            P(None, "fsdp", None),
            P(None, "fsdp"),
            P(None, "fsdp", None),
            P(None, "fsdp"),
            P(None, "fsdp", None),
            P(None, "fsdp", None),
            P(None, "fsdp", None),
        ),
        check_vma=False,
    )
```
